32 devices in a mesh: groups: 2 (over x), blocks: 16 (over z, y, core).
Axes of the slice: x: 2, y: 2, z: 4, core: 2. Of those that a mesh axis runs over, the one named last changes fastest.
Arguments:
- estimate: float32 [512, 128, 128], P(('groups', 'blocks')), parts along dimension 0, may hold values from 0.5 to 1.5
- images: bfloat16 [8, 512, 128, 128], P(None, ('groups', 'blocks')), parts along dimension 1, may hold values from 0.25 to 2
- point_spread: float32 [8, 3, 31], replicated, may hold values from 0.05 to 1
- shifts: int32 [8], replicated, may hold values from -32 to 32, as said below
Outputs:
- restored: float32 [512, 128, 128], P(('groups', 'blocks')), parts along dimension 0
The draws below stay inside these ranges and needn't reach their ends.
There are 2 independent parts, one for each index of `groups`. The reference program is written for one: setup_inputs(seed, part) draws one part's arguments, and reference() takes and returns one part's arrays. A program takes and returns all parts, laid end to end along the dimension named above; an argument that names none is the same for every part. Nothing has to cross between parts.
Inputs may be any that keep to these rules, and one draw needn't show every extreme that they name: `shifts`: one view is placed at exactly 32 and another at exactly -32.
All inputs are finite; a program needn't handle non-finite values.
Results may differ from the reference program's by a relative error of at most 0.00031.
Values may be sent and summed in bfloat16 or wider, within the bound.
A program may use at most 128 MiB of HBM per device.

```python
import math
import jax
import jax.numpy as jnp
from jax import lax

VIEWS = 8
TAPS = 31
NY = 128
NZ = 128
ITERS = 1
SLAB = 256
SHIFT = 32


def draw_shifts(key, part):
    first_key, second_key = jax.random.split(key)
    values = jax.random.randint(first_key, (VIEWS,), 0 - SHIFT, SHIFT + 1)
    order = jax.random.permutation(second_key, VIEWS)
    values = values.at[order[0]].set(SHIFT)
    values = values.at[order[1]].set(0 - SHIFT)
    return values.astype(jnp.int32)


def block_scale(own_key, shape, pieces, smallest, top_value):
    def one(dim, parts):
        steps = jax.random.uniform(jax.random.fold_in(jax.random.fold_in(own_key, 6), dim), (parts,), jnp.float32, smallest / len(pieces), top_value / len(pieces))
        return jnp.repeat(jnp.exp(steps), shape[dim] // parts).reshape((-1,) + (1,) * (len(shape) - dim - 1))

    level = one(*pieces[0])
    for cut in pieces[1:]:
        level = level * one(*cut)
    return level


def setup_inputs(seed: int = 0, part: int = 0) -> dict:
    key_of = jax.random.split(jax.random.key(seed), 5)
    own_keys = jax.random.split(jax.random.fold_in(key_of[4], part), 5)
    return {
        "estimate": jnp.clip(0.5 + 1.0 * jax.random.uniform(own_keys[0], (SLAB, NY, NZ), jnp.float32) ** block_scale(own_keys[0], (SLAB, NY, NZ), ((0, 16),), -0.2, 0.2), 0.5, 1.5),
        "images": jnp.clip(0.25 + 1.75 * jax.random.uniform(own_keys[1], (VIEWS, SLAB, NY, NZ), jnp.float32) ** block_scale(own_keys[1], (VIEWS, SLAB, NY, NZ), ((1, 16),), -0.2, 0.2), 0.25, 2.0).astype(jnp.bfloat16),
        "point_spread": jnp.clip(jnp.exp(jax.random.uniform(key_of[2], (VIEWS, 3, TAPS), jnp.float32, math.log(0.05), math.log(1.0))), 0.05, 1.0),
        "shifts": draw_shifts(jax.random.fold_in(key_of[4], 71), part),
    }


def banded(tap_values, count_in, count_out, offset, direction):
    row_index = jnp.arange(count_in)[:, None]
    col_index = jnp.arange(count_out)[None, :]
    position = direction * (row_index - col_index) + offset
    matches = position[:, :, None] == jnp.arange(tap_values.shape[0])[None, None, :]
    spread = jnp.where(matches, tap_values.astype(jnp.float32)[None, None, :], jnp.float32(0.0))
    return jnp.sum(spread, axis=2).astype(jnp.bfloat16)


def forward_x(blurred, tap_values):
    margin = tap_values.shape[0] // 2
    slab_rows = blurred.shape[0]
    padded = jnp.pad(blurred.astype(jnp.float32), ((margin, margin), (0, 0), (0, 0)))
    summed = jnp.zeros(blurred.shape, jnp.float32)
    for tap in range(tap_values.shape[0]):
        summed = summed + tap_values[tap].astype(jnp.float32) * padded[tap:tap + slab_rows]
    return summed


def adjoint_x(quotient, tap_values):
    margin = tap_values.shape[0] // 2
    slab_rows = quotient.shape[0]
    padded = jnp.pad(quotient.astype(jnp.float32), ((margin, margin), (0, 0), (0, 0)))
    summed = jnp.zeros(quotient.shape, jnp.float32)
    for tap in range(tap_values.shape[0]):
        start = 2 * margin - tap
        summed = summed + tap_values[tap].astype(jnp.float32) * padded[start:start + slab_rows]
    return summed


def reference(estimate, images, point_spread, shifts):
    kernel = (point_spread / jnp.sum(point_spread, axis=2, keepdims=True)).astype(jnp.bfloat16)
    slab_rows = estimate.shape[0]
    padded = jnp.pad(images, ((0, 0), (SHIFT, SHIFT), (0, 0), (0, 0)))
    aligned = []
    for view in range(VIEWS):
        start = (SHIFT + shifts[view]).astype(jnp.int32)
        aligned.append(lax.dynamic_slice_in_dim(padded[view], start, slab_rows, 0))
    current = estimate
    for sweep in range(ITERS):
        current_b = current.astype(jnp.bfloat16)
        summed = jnp.zeros(estimate.shape, jnp.float32)
        for view in range(VIEWS):
            z_matrix = banded(kernel[view, 2], NZ, NZ, 15, 1)
            y_matrix = banded(kernel[view, 1], NY, NY, 15, 1)
            blur_z = jnp.dot(current_b.reshape(-1, NZ), z_matrix, preferred_element_type=jnp.float32)
            blur_z = blur_z.astype(jnp.bfloat16).reshape(slab_rows, NY, NZ)
            blur_y = jnp.einsum('xyz,yk->xkz', blur_z.astype(jnp.float32), y_matrix.astype(jnp.float32)).astype(jnp.bfloat16)
            predicted = forward_x(blur_y, kernel[view, 0])
            quotient = (aligned[view].astype(jnp.float32) / predicted).astype(jnp.bfloat16)
            back_x = adjoint_x(quotient, kernel[view, 0]).astype(jnp.bfloat16)
            back_y = jnp.einsum('xkz,yk->xyz', back_x.astype(jnp.float32), y_matrix.astype(jnp.float32)).astype(jnp.bfloat16)
            correction = jnp.dot(back_y.reshape(-1, NZ), z_matrix.T, preferred_element_type=jnp.float32)
            summed = summed + correction.reshape(slab_rows, NY, NZ)
        current = current * summed / VIEWS
    return current
```

```python
import functools

import jax
import jax.numpy as jnp
from jax import lax
from jax.experimental import pallas as pl
from jax.experimental.pallas import tpu as pltpu
from jax.sharding import PartitionSpec as P

SHIFT = 32
F32 = jnp.float32
BF16 = jnp.bfloat16
HALF = jnp.float16
MESH = pl.DeviceIdType.MESH


def moved(value, axis, steps):
    count = lax.axis_size(axis)
    pairs = [(source, source + steps) for source in range(count) if 0 <= source + steps < count]
    return lax.ppermute(value, axis, pairs)


def greet(count, me, hops):
    barrier = pltpu.get_barrier_semaphore()
    for k in range(1, hops + 1):
        for step in (k, -k):
            there = me + step

            @pl.when((there >= 0) & (there < count))
            def _():
                pl.semaphore_signal(
                    barrier, inc=1, device_id={"blocks": there}, device_id_type=MESH
                )

    pl.semaphore_wait(barrier, jnp.minimum(me, hops) + jnp.minimum(count - 1 - me, hops))


def window_kernel(count, hops, own_ref, out_ref, send_sem, recv_sem):
    me = lax.axis_index("blocks")
    greet(count, me, hops)
    order = [s for k in range(hops, 0, -1) for s in (k, -k)]

    def copy(step):
        return pltpu.make_async_remote_copy(
            src_ref=own_ref,
            dst_ref=out_ref.at[hops - step],
            send_sem=send_sem.at[hops - step],
            recv_sem=recv_sem.at[hops - step],
            device_id={"blocks": me + step},
            device_id_type=MESH,
        )

    for step in order:
        there = me + step

        @pl.when((there >= 0) & (there < count))
        def _():
            copy(step).start()

    out_ref[hops] = own_ref[...]
    for step in order:
        here = me - step

        @pl.when((here < 0) | (here >= count))
        def _():
            out_ref[hops - step] = jnp.zeros(own_ref.shape, own_ref.dtype)

    for step in order:
        there = me + step
        here = me - step

        @pl.when((there >= 0) & (there < count))
        def _():
            copy(step).wait_send()

        @pl.when((here >= 0) & (here < count))
        def _():
            copy(step).wait_recv()


def view_kernel(
    dims, win_ref, img_ref, xm_ref, xt_ref, tap_ref, extra_ref, own_ref, part_ref, held, low, mats
):
    views, rows, across, along, hops, margin = dims
    group = 16
    r = lax.broadcasted_iota(jnp.int32, (along, along), 0)
    c = lax.broadcasted_iota(jnp.int32, (along, along), 1)
    near = jnp.abs(r - c) <= margin

    @pl.loop(0, views)
    def _(v):
        for kind in range(4):
            line = jnp.broadcast_to(tap_ref[v, pl.ds(kind, 1), :], (along, along))
            turned = pltpu.roll(line, 0, 1, stride=1, stride_axis=0)
            mats[v, kind] = jnp.where(near, turned, 0.0).astype(BF16)

    @pl.loop(0, across // group)
    def _(g):
        base = pl.multiple_of(g * group, group)
        slabs = []
        for p in range(group):
            piece = win_ref[:, base + p].reshape(win_ref.shape[0] * rows, along)
            slabs.append(jnp.dot(xm_ref[...], piece, preferred_element_type=F32).astype(BF16))
        held[:, pl.ds(base, group), :] = jnp.swapaxes(jnp.stack(slabs), 0, 1)

    some = 4
    per = rows // some

    def both(left, block):
        outs = []
        for i in range(0, some, 2):
            pair = jnp.concatenate([block[i], block[i + 1]], axis=1)
            res = jnp.dot(left, pair, preferred_element_type=F32)
            outs += [res[:, :along], res[:, along:]]
        return outs

    @pl.loop(0, views * per)
    def _(t):
        v = t // per
        first = pl.multiple_of(t * some, some)
        inside = (t % per) * some
        block = held[pl.ds(first, some)].reshape(some * across, along)
        blur_z = jnp.dot(block, mats[v, 0], preferred_element_type=F32).astype(BF16)
        predicted = both(mats[v, 2], blur_z.reshape(some, across, along))
        ratios = []
        for i in range(some):
            image = img_ref[v, inside + i].astype(F32)
            ratios.append((image / (predicted[i] + extra_ref[first + i])).astype(BF16))
        ratio = jnp.concatenate(ratios, axis=0)
        back_z = jnp.dot(ratio, mats[v, 1], preferred_element_type=F32).astype(BF16)
        back = both(mats[v, 3], back_z.reshape(some, across, along))
        for i in range(some):
            top = back[i].astype(BF16)
            held[first + i] = top
            low[first + i] = (back[i] - top.astype(F32)).astype(BF16)

    @pl.loop(0, across // group)
    def _(g):
        base = pl.multiple_of(g * group, group)
        tops = jnp.swapaxes(held[:, pl.ds(base, group), :], 0, 1)
        lows = jnp.swapaxes(low[:, pl.ds(base, group), :], 0, 1)
        for p in range(group):
            stacked = jnp.concatenate([tops[p], lows[p]], axis=0)
            res = jnp.dot(xt_ref[...], stacked, preferred_element_type=F32)
            res = res.reshape(2 * hops + 1, rows, along)
            own_ref[base + p] = res[hops]
            for k in range(hops):
                part_ref[k, base + p] = res[k].astype(part_ref.dtype)
                part_ref[hops + k, base + p] = res[hops + 1 + k].astype(part_ref.dtype)


def vmem(n):
    return [pl.BlockSpec(memory_space=pltpu.VMEM)] * n


def taken(taps, index):
    match = index[..., None] == jnp.arange(taps.shape[-1])
    return jnp.sum(jnp.where(match, taps.astype(F32), 0.0), axis=-1)


def body(estimate, images, point_spread, shifts):
    views = images.shape[0]
    rows, across, along = estimate.shape
    taps = point_spread.shape[2]
    margin = taps // 2
    count = lax.axis_size("blocks")
    hops = -(-(margin + SHIFT) // rows)
    width = rows * (2 * hops + 1)
    slab = rows * count
    kernel = (point_spread / jnp.sum(point_spread, axis=2, keepdims=True)).astype(BF16)

    place = (jnp.arange(along) + along // 2) % along - along // 2
    plus = margin + place
    minus = margin - place
    lines = jnp.stack([minus, plus, plus, minus])
    which = jnp.stack([kernel[:, 2], kernel[:, 2], kernel[:, 1], kernel[:, 1]], axis=1)
    tap_lines = taken(which[:, :, None, :], lines[None])

    own = lax.axis_index("blocks") * rows + jnp.arange(rows)[None, :] - shifts[:, None]
    valid = (own >= 0) & (own < slab)
    index = (
        jnp.arange(width)[None, None, :]
        - jnp.arange(rows)[None, :, None]
        + shifts[:, None, None]
        + (margin - rows * hops)
    )
    x_mat = jnp.where(valid[:, :, None], taken(kernel[:, 0][:, None, None, :], index), 0.0)
    x_mat = x_mat.astype(BF16).reshape(views * rows, width)
    x_turned = x_mat.T
    x_twice = jnp.concatenate([x_turned, x_turned], axis=1)
    extra = jnp.where(valid, 0.0, 1.0).astype(F32).reshape(views * rows)

    block = (across, rows, along)
    mine = jnp.swapaxes(estimate.astype(BF16), 0, 1)
    window = pl.pallas_call(
        functools.partial(window_kernel, count, hops),
        out_shape=jax.ShapeDtypeStruct((2 * hops + 1,) + block, BF16),
        in_specs=vmem(1),
        out_specs=vmem(1)[0],
        scratch_shapes=[
            pltpu.SemaphoreType.DMA((2 * hops + 1,)),
            pltpu.SemaphoreType.DMA((2 * hops + 1,)),
        ],
        compiler_params=pltpu.CompilerParams(collective_id=0, has_side_effects=True),
        name="window",
    )(mine)

    dims = (views, rows, across, along, hops, margin)
    own_sum, parts = pl.pallas_call(
        functools.partial(view_kernel, dims),
        out_shape=(
            jax.ShapeDtypeStruct(block, F32),
            jax.ShapeDtypeStruct((2 * hops,) + block, F32),
        ),
        in_specs=vmem(5) + [pl.BlockSpec(memory_space=pltpu.SMEM)],
        out_specs=tuple(vmem(2)),
        scratch_shapes=[
            pltpu.VMEM((views * rows, across, along), BF16),
            pltpu.VMEM((views * rows, across, along), BF16),
            pltpu.VMEM((views, 4, along, along), BF16),
        ],
        compiler_params=pltpu.CompilerParams(vmem_limit_bytes=56 * 1024 * 1024),
        name="views",
    )(window, images, x_mat, x_twice, tap_lines, extra)

    sent = parts.astype(HALF)
    summed = own_sum
    for k in range(hops):
        summed = summed + moved(sent[hops + k], "blocks", k + 1).astype(F32)
        summed = summed + moved(sent[hops - 1 - k], "blocks", -k - 1).astype(F32)
    return estimate * jnp.swapaxes(summed, 0, 1) / views


def solution(mesh):
    in_specs = (
        P(("groups", "blocks"), None, None),
        P(None, ("groups", "blocks"), None, None),
        P(),
        P(),
    )
    out_specs = P(("groups", "blocks"), None, None)
    return jax.shard_map(body, mesh=mesh, in_specs=in_specs, out_specs=out_specs, check_vma=False)
```

```python
import functools

import jax
import jax.numpy as jnp
from jax import lax
from jax.experimental import pallas as pl
from jax.experimental.pallas import tpu as pltpu
from jax.sharding import PartitionSpec as P

SHIFT = 32
F32 = jnp.float32
BF16 = jnp.bfloat16
HALF = jnp.float16
MESH = pl.DeviceIdType.MESH


def window_kernel(count, own_ref, out_ref, send_sem, recv_sem):
    me = lax.axis_index("blocks")
    odd = lax.rem(me, 2)
    mid = 3

    def send(src, slot, there, sem):
        return pltpu.make_async_remote_copy(
            src_ref=src,
            dst_ref=out_ref.at[slot],
            send_sem=send_sem.at[sem],
            recv_sem=recv_sem.at[slot],
            device_id={"blocks": there},
            device_id_type=MESH,
        )

    def run(mate, far):
        low = me >= 2
        high = me + 2 < count
        away = (me + far >= 0) & (me + far < count)
        barrier = pltpu.get_barrier_semaphore()

        def signal(there):
            pl.semaphore_signal(barrier, inc=1, device_id={"blocks": there}, device_id_type=MESH)

        signal(me + mate)
        pl.when(low)(lambda: signal(me - 2))
        pl.when(high)(lambda: signal(me + 2))
        pl.when(away)(lambda: signal(me + far))
        peers = 1 + low.astype(jnp.int32) + high.astype(jnp.int32) + away.astype(jnp.int32)
        pl.semaphore_wait(barrier, peers)

        down = send(own_ref, mid + 2, me - 2, 0)
        up = send(own_ref, mid - 2, me + 2, 1)
        long = send(own_ref, mid - far, me + far, 2)
        near = send(own_ref, mid - mate, me + mate, 3)
        pass_low = send(out_ref.at[mid - 2], mid - 2 - mate, me + mate, 4)
        pass_high = send(out_ref.at[mid + 2], mid + 2 - mate, me + mate, 5)
        pl.when(low)(down.start)
        pl.when(high)(up.start)
        pl.when(away)(long.start)
        near.start()

        out_ref[mid] = own_ref[...]
        for offset in (-3, -2, -1, 1, 2, 3):
            if offset != mate:
                there = me + offset

                @pl.when((there < 0) | (there >= count))
                def _():
                    out_ref[mid + offset] = jnp.zeros(own_ref.shape, own_ref.dtype)

        @pl.when(low)
        def _():
            up.wait_recv()
            pass_low.start()

        @pl.when(high)
        def _():
            down.wait_recv()
            pass_high.start()

        send(own_ref, mid + mate, me + mate, 3).wait_recv()

        @pl.when(low)
        def _():
            send(own_ref, mid - 2 + mate, me + mate, 4).wait_recv()
            pass_low.wait_send()
            down.wait_send()

        @pl.when(high)
        def _():
            send(own_ref, mid + 2 + mate, me + mate, 5).wait_recv()
            pass_high.wait_send()
            up.wait_send()

        @pl.when(away)
        def _():
            send(own_ref, mid + far, me + far, 2).wait_recv()
            long.wait_send()

        near.wait_send()

    pl.when(odd == 0)(lambda: run(1, -3))
    pl.when(odd == 1)(lambda: run(-1, 3))


def view_kernel(
    dims, win_ref, img_ref, xm_ref, xt_ref, tap_ref, extra_ref, odd_ref, keep_ref, mate_ref, far_ref, held, low, mats
):
    views, rows, across, along, hops, margin = dims
    group = 16
    r = lax.broadcasted_iota(jnp.int32, (along, along), 0)
    c = lax.broadcasted_iota(jnp.int32, (along, along), 1)
    near = jnp.abs(r - c) <= margin

    @pl.loop(0, views)
    def _(v):
        for kind in range(4):
            line = jnp.broadcast_to(tap_ref[v, pl.ds(kind, 1), :], (along, along))
            turned = pltpu.roll(line, 0, 1, stride=1, stride_axis=0)
            mats[v, kind] = jnp.where(near, turned, 0.0).astype(BF16)

    @pl.loop(0, across // group)
    def _(g):
        base = pl.multiple_of(g * group, group)
        slabs = []
        for p in range(group):
            piece = win_ref[:, base + p].reshape(win_ref.shape[0] * rows, along)
            slabs.append(jnp.dot(xm_ref[...], piece, preferred_element_type=F32).astype(BF16))
        held[:, pl.ds(base, group), :] = jnp.swapaxes(jnp.stack(slabs), 0, 1)

    some = 4
    per = rows // some

    def both(left, block):
        outs = []
        for i in range(0, some, 2):
            pair = jnp.concatenate([block[i], block[i + 1]], axis=1)
            res = jnp.dot(left, pair, preferred_element_type=F32)
            outs += [res[:, :along], res[:, along:]]
        return outs

    @pl.loop(0, views * per)
    def _(t):
        v = t // per
        first = pl.multiple_of(t * some, some)
        inside = (t % per) * some
        block = held[pl.ds(first, some)].reshape(some * across, along)
        blur_z = jnp.dot(block, mats[v, 0], preferred_element_type=F32).astype(BF16)
        predicted = both(mats[v, 2], blur_z.reshape(some, across, along))
        ratios = []
        for i in range(some):
            image = img_ref[v, inside + i].astype(F32)
            ratios.append((image / (predicted[i] + extra_ref[first + i])).astype(BF16))
        ratio = jnp.concatenate(ratios, axis=0)
        back_z = jnp.dot(ratio, mats[v, 1], preferred_element_type=F32).astype(BF16)
        back = both(mats[v, 3], back_z.reshape(some, across, along))
        for i in range(some):
            top = back[i].astype(BF16)
            held[first + i] = top
            low[first + i] = (back[i] - top.astype(F32)).astype(BF16)

    @pl.loop(0, across // group)
    def _(g):
        base = pl.multiple_of(g * group, group)
        tops = jnp.swapaxes(held[:, pl.ds(base, group), :], 0, 1)
        lows = jnp.swapaxes(low[:, pl.ds(base, group), :], 0, 1)
        for p in range(group):
            stacked = jnp.concatenate([tops[p], lows[p]], axis=0)
            res = jnp.dot(xt_ref[...], stacked, preferred_element_type=F32)
            res = res.reshape(2 * hops + 1, rows, along)
            for k in range(3):
                keep_ref[k, base + p] = res[2 * k + 1]

            @pl.when(odd_ref[0] == 0)
            def _():
                for k in range(3):
                    mate_ref[k, base + p] = res[2 * k + 2]
                far_ref[base + p] = res[0]

            @pl.when(odd_ref[0] == 1)
            def _():
                for k in range(3):
                    mate_ref[k, base + p] = res[2 * k]
                far_ref[base + p] = res[6]


def vmem(n):
    return [pl.BlockSpec(memory_space=pltpu.VMEM)] * n


def taken(taps, index):
    match = index[..., None] == jnp.arange(taps.shape[-1])
    return jnp.sum(jnp.where(match, taps.astype(F32), 0.0), axis=-1)


def body(estimate, images, point_spread, shifts):
    views = images.shape[0]
    rows, across, along = estimate.shape
    taps = point_spread.shape[2]
    margin = taps // 2
    count = lax.axis_size("blocks")
    hops = -(-(margin + SHIFT) // rows)
    width = rows * (2 * hops + 1)
    slab = rows * count
    kernel = (point_spread / jnp.sum(point_spread, axis=2, keepdims=True)).astype(BF16)

    place = (jnp.arange(along) + along // 2) % along - along // 2
    plus = margin + place
    minus = margin - place
    lines = jnp.stack([minus, plus, plus, minus])
    which = jnp.stack([kernel[:, 2], kernel[:, 2], kernel[:, 1], kernel[:, 1]], axis=1)
    tap_lines = taken(which[:, :, None, :], lines[None])

    own = lax.axis_index("blocks") * rows + jnp.arange(rows)[None, :] - shifts[:, None]
    valid = (own >= 0) & (own < slab)
    index = (
        jnp.arange(width)[None, None, :]
        - jnp.arange(rows)[None, :, None]
        + shifts[:, None, None]
        + (margin - rows * hops)
    )
    x_mat = jnp.where(valid[:, :, None], taken(kernel[:, 0][:, None, None, :], index), 0.0)
    x_mat = x_mat.astype(BF16).reshape(views * rows, width)
    x_turned = x_mat.T
    x_twice = jnp.concatenate([x_turned, x_turned], axis=1)
    extra = jnp.where(valid, 0.0, 1.0).astype(F32).reshape(views * rows)

    odd = lax.rem(lax.axis_index("blocks"), 2).astype(jnp.int32).reshape(1)

    block = (across, rows, along)
    mine = jnp.swapaxes(estimate.astype(BF16), 0, 1)
    window = pl.pallas_call(
        functools.partial(window_kernel, count),
        out_shape=jax.ShapeDtypeStruct((2 * hops + 1,) + block, BF16),
        in_specs=vmem(1),
        out_specs=vmem(1)[0],
        scratch_shapes=[
            pltpu.SemaphoreType.DMA((2 * hops + 1,)),
            pltpu.SemaphoreType.DMA((2 * hops + 1,)),
        ],
        compiler_params=pltpu.CompilerParams(collective_id=0, has_side_effects=True),
        name="window",
    )(mine)

    dims = (views, rows, across, along, hops, margin)
    keep, mates, far = pl.pallas_call(
        functools.partial(view_kernel, dims),
        out_shape=(
            jax.ShapeDtypeStruct((3,) + block, F32),
            jax.ShapeDtypeStruct((3,) + block, F32),
            jax.ShapeDtypeStruct(block, F32),
        ),
        in_specs=vmem(5) + [pl.BlockSpec(memory_space=pltpu.SMEM)] * 2,
        out_specs=tuple(vmem(3)),
        scratch_shapes=[
            pltpu.VMEM((views * rows, across, along), BF16),
            pltpu.VMEM((views * rows, across, along), BF16),
            pltpu.VMEM((views, 4, along, along), BF16),
        ],
        compiler_params=pltpu.CompilerParams(vmem_limit_bytes=56 * 1024 * 1024),
        name="views",
    )(window, images, x_mat, x_twice, tap_lines, extra, odd)


    def sent(value, step_of):
        pairs = [(i, i + step_of(i)) for i in range(count) if 0 <= i + step_of(i) < count]
        return lax.ppermute(value.astype(HALF), "blocks", pairs).astype(F32)

    away = sent(far, lambda i: 3 if i % 2 else -3)
    keep = keep + sent(mates, lambda i: -1 if i % 2 else 1)
    summed = keep[1] + away + sent(keep[0], lambda i: -2) + sent(keep[2], lambda i: 2)
    return estimate * jnp.swapaxes(summed, 0, 1) / views


def solution(mesh):
    in_specs = (
        P(("groups", "blocks"), None, None),
        P(None, ("groups", "blocks"), None, None),
        P(),
        P(),
    )
    out_specs = P(("groups", "blocks"), None, None)
    return jax.shard_map(body, mesh=mesh, in_specs=in_specs, out_specs=out_specs, check_vma=False)
```

```python
import functools

import jax
import jax.numpy as jnp
from jax import lax
from jax.experimental import pallas as pl
from jax.experimental.pallas import tpu as pltpu
from jax.sharding import PartitionSpec as P

SHIFT = 32
PARTS = 4
F32 = jnp.float32
BF16 = jnp.bfloat16
HALF = jnp.float16
MESH = pl.DeviceIdType.MESH


def window_kernel(count, own_ref, out_ref, send_sem, recv_sem):
    me = lax.axis_index("blocks")
    odd = lax.rem(me, 2)
    mid = 3

    part = own_ref.shape[0] // PARTS

    def send(src, slot, there, sem, j):
        span = pl.ds(j * part, part)
        return pltpu.make_async_remote_copy(
            src_ref=src.at[span],
            dst_ref=out_ref.at[slot, span],
            send_sem=send_sem.at[sem, j],
            recv_sem=recv_sem.at[slot, j],
            device_id={"blocks": there},
            device_id_type=MESH,
        )

    def run(mate, far):
        low = me >= 2
        high = me + 2 < count
        away = (me + far >= 0) & (me + far < count)
        barrier = pltpu.get_barrier_semaphore()

        def signal(there):
            pl.semaphore_signal(barrier, inc=1, device_id={"blocks": there}, device_id_type=MESH)

        signal(me + mate)
        pl.when(low)(lambda: signal(me - 2))
        pl.when(high)(lambda: signal(me + 2))
        pl.when(away)(lambda: signal(me + far))
        peers = 1 + low.astype(jnp.int32) + high.astype(jnp.int32) + away.astype(jnp.int32)
        pl.semaphore_wait(barrier, peers)

        def down(j):
            return send(own_ref, mid + 2, me - 2, 0, j)

        def up(j):
            return send(own_ref, mid - 2, me + 2, 1, j)

        def long(j):
            return send(own_ref, mid - far, me + far, 2, j)

        def near(j):
            return send(own_ref, mid - mate, me + mate, 3, j)

        def pass_low(j):
            return send(out_ref.at[mid - 2], mid - 2 - mate, me + mate, 4, j)

        def pass_high(j):
            return send(out_ref.at[mid + 2], mid + 2 - mate, me + mate, 5, j)

        for j in range(PARTS):
            pl.when(low)(lambda: down(j).start())
            pl.when(high)(lambda: up(j).start())
            near(j).start()
        for j in range(PARTS):
            pl.when(away)(lambda: long(j).start())

        out_ref[mid] = own_ref[...]
        for offset in (-3, -2, -1, 1, 2, 3):
            if offset != mate:
                there = me + offset

                @pl.when((there < 0) | (there >= count))
                def _():
                    out_ref[mid + offset] = jnp.zeros(own_ref.shape, own_ref.dtype)

        for j in range(PARTS):

            @pl.when(low)
            def _():
                up(j).wait_recv()
                pass_low(j).start()

            @pl.when(high)
            def _():
                down(j).wait_recv()
                pass_high(j).start()

        for j in range(PARTS):
            send(own_ref, mid + mate, me + mate, 3, j).wait_recv()

            @pl.when(low)
            def _():
                send(own_ref, mid - 2 + mate, me + mate, 4, j).wait_recv()
                pass_low(j).wait_send()
                down(j).wait_send()

            @pl.when(high)
            def _():
                send(own_ref, mid + 2 + mate, me + mate, 5, j).wait_recv()
                pass_high(j).wait_send()
                up(j).wait_send()

            @pl.when(away)
            def _():
                send(own_ref, mid + far, me + far, 2, j).wait_recv()
                long(j).wait_send()

            near(j).wait_send()

    pl.when(odd == 0)(lambda: run(1, -3))
    pl.when(odd == 1)(lambda: run(-1, 3))


def view_kernel(
    dims, win_ref, img_ref, xm_ref, xt_ref, tap_ref, extra_ref, keep_ref, mate_ref, far_ref, held, low, mats
):
    views, rows, across, along, hops, margin = dims
    group = 16
    r = lax.broadcasted_iota(jnp.int32, (along, along), 0)
    c = lax.broadcasted_iota(jnp.int32, (along, along), 1)
    near = jnp.abs(r - c) <= margin

    @pl.loop(0, views)
    def _(v):
        for kind in range(4):
            line = jnp.broadcast_to(tap_ref[v, pl.ds(kind, 1), :], (along, along))
            turned = pltpu.roll(line, 0, 1, stride=1, stride_axis=0)
            mats[v, kind] = jnp.where(near, turned, 0.0).astype(BF16)

    @pl.loop(0, across // group)
    def _(g):
        base = pl.multiple_of(g * group, group)
        slabs = []
        for p in range(group):
            piece = win_ref[:, base + p].reshape(win_ref.shape[0] * rows, along)
            slabs.append(jnp.dot(xm_ref[...], piece, preferred_element_type=F32).astype(BF16))
        held[:, pl.ds(base, group), :] = jnp.swapaxes(jnp.stack(slabs), 0, 1)

    some = 4
    per = rows // some

    def both(left, block):
        outs = []
        for i in range(0, some, 2):
            pair = jnp.concatenate([block[i], block[i + 1]], axis=1)
            res = jnp.dot(left, pair, preferred_element_type=F32)
            outs += [res[:, :along], res[:, along:]]
        return outs

    @pl.loop(0, views * per)
    def _(t):
        v = t // per
        first = pl.multiple_of(t * some, some)
        inside = (t % per) * some
        block = held[pl.ds(first, some)].reshape(some * across, along)
        blur_z = jnp.dot(block, mats[v, 0], preferred_element_type=F32).astype(BF16)
        predicted = both(mats[v, 2], blur_z.reshape(some, across, along))
        ratios = []
        for i in range(some):
            image = img_ref[v, inside + i].astype(F32)
            ratios.append((image / (predicted[i] + extra_ref[first + i])).astype(BF16))
        ratio = jnp.concatenate(ratios, axis=0)
        back_z = jnp.dot(ratio, mats[v, 1], preferred_element_type=F32).astype(BF16)
        back = both(mats[v, 3], back_z.reshape(some, across, along))
        for i in range(some):
            top = back[i].astype(BF16)
            held[first + i] = top
            low[first + i] = (back[i] - top.astype(F32)).astype(BF16)

    @pl.loop(0, across // group)
    def _(g):
        base = pl.multiple_of(g * group, group)
        tops = jnp.swapaxes(held[:, pl.ds(base, group), :], 0, 1)
        lows = jnp.swapaxes(low[:, pl.ds(base, group), :], 0, 1)
        for p in range(group):
            stacked = jnp.concatenate([tops[p], lows[p]], axis=0)
            res = jnp.dot(xt_ref[...], stacked, preferred_element_type=F32)
            res = res.reshape(2 * hops + 1, rows, along)
            for k in range(3):
                keep_ref[k, base + p] = res[k]
                mate_ref[k, base + p] = res[3 + k]
            far_ref[base + p] = res[6]


def vmem(n):
    return [pl.BlockSpec(memory_space=pltpu.VMEM)] * n


def taken(taps, index):
    match = index[..., None] == jnp.arange(taps.shape[-1])
    return jnp.sum(jnp.where(match, taps.astype(F32), 0.0), axis=-1)


def body(estimate, images, point_spread, shifts):
    views = images.shape[0]
    rows, across, along = estimate.shape
    taps = point_spread.shape[2]
    margin = taps // 2
    count = lax.axis_size("blocks")
    hops = -(-(margin + SHIFT) // rows)
    width = rows * (2 * hops + 1)
    slab = rows * count
    kernel = (point_spread / jnp.sum(point_spread, axis=2, keepdims=True)).astype(BF16)

    place = (jnp.arange(along) + along // 2) % along - along // 2
    plus = margin + place
    minus = margin - place
    lines = jnp.stack([minus, plus, plus, minus])
    which = jnp.stack([kernel[:, 2], kernel[:, 2], kernel[:, 1], kernel[:, 1]], axis=1)
    tap_lines = taken(which[:, :, None, :], lines[None])

    own = lax.axis_index("blocks") * rows + jnp.arange(rows)[None, :] - shifts[:, None]
    valid = (own >= 0) & (own < slab)
    index = (
        jnp.arange(width)[None, None, :]
        - jnp.arange(rows)[None, :, None]
        + shifts[:, None, None]
        + (margin - rows * hops)
    )
    x_mat = jnp.where(valid[:, :, None], taken(kernel[:, 0][:, None, None, :], index), 0.0)
    x_mat = x_mat.astype(BF16).reshape(views * rows, width)
    odd = lax.axis_index("blocks") % 2
    order = jnp.where(odd == 1, jnp.array([1, 3, 5, 0, 2, 4, 6]), jnp.array([1, 3, 5, 2, 4, 6, 0]))
    x_turned = x_mat.T.reshape(2 * hops + 1, rows, views * rows)[order].reshape(width, views * rows)
    x_twice = jnp.concatenate([x_turned, x_turned], axis=1)
    extra = jnp.where(valid, 0.0, 1.0).astype(F32).reshape(views * rows)

    block = (across, rows, along)
    mine = jnp.swapaxes(estimate.astype(BF16), 0, 1)
    window = pl.pallas_call(
        functools.partial(window_kernel, count),
        out_shape=jax.ShapeDtypeStruct((2 * hops + 1,) + block, BF16),
        in_specs=vmem(1),
        out_specs=vmem(1)[0],
        scratch_shapes=[
            pltpu.SemaphoreType.DMA((6, PARTS)),
            pltpu.SemaphoreType.DMA((2 * hops + 1, PARTS)),
        ],
        compiler_params=pltpu.CompilerParams(collective_id=0, has_side_effects=True),
        name="window",
    )(mine)

    dims = (views, rows, across, along, hops, margin)
    keep, mates, far = pl.pallas_call(
        functools.partial(view_kernel, dims),
        out_shape=(
            jax.ShapeDtypeStruct((3,) + block, F32),
            jax.ShapeDtypeStruct((3,) + block, F32),
            jax.ShapeDtypeStruct(block, F32),
        ),
        in_specs=vmem(5) + [pl.BlockSpec(memory_space=pltpu.SMEM)],
        out_specs=tuple(vmem(3)),
        scratch_shapes=[
            pltpu.VMEM((views * rows, across, along), BF16),
            pltpu.VMEM((views * rows, across, along), BF16),
            pltpu.VMEM((views, 4, along, along), BF16),
        ],
        compiler_params=pltpu.CompilerParams(vmem_limit_bytes=56 * 1024 * 1024),
        name="views",
    )(window, images, x_mat, x_twice, tap_lines, extra)


    def sent(value, step_of):
        pairs = [(i, i + step_of(i)) for i in range(count) if 0 <= i + step_of(i) < count]
        return lax.ppermute(value.astype(HALF), "blocks", pairs).astype(F32)

    away = sent(far, lambda i: 3 if i % 2 else -3)
    keep = keep + sent(mates, lambda i: -1 if i % 2 else 1)
    summed = keep[1] + away + sent(keep[0], lambda i: -2) + sent(keep[2], lambda i: 2)
    return estimate * jnp.swapaxes(summed, 0, 1) / views


def solution(mesh):
    in_specs = (
        P(("groups", "blocks"), None, None),
        P(None, ("groups", "blocks"), None, None),
        P(),
        P(),
    )
    out_specs = P(("groups", "blocks"), None, None)
    return jax.shard_map(body, mesh=mesh, in_specs=in_specs, out_specs=out_specs, check_vma=False)
```

```python
import functools

import jax
import jax.numpy as jnp
from jax import lax
from jax.experimental import pallas as pl
from jax.experimental.pallas import tpu as pltpu
from jax.sharding import PartitionSpec as P

SHIFT = 32
PARTS = 4
F32 = jnp.float32
BF16 = jnp.bfloat16
HALF = jnp.float16
MESH = pl.DeviceIdType.MESH


def window_kernel(count, own_ref, out_ref, send_sem, recv_sem):
    me = lax.axis_index("blocks")
    odd = lax.rem(me, 2)
    right = lax.rem(me, 4) >= 2
    mid = 3

    part = own_ref.shape[0] // PARTS

    def send(src, slot, there, sem, j):
        span = pl.ds(j * part, part)
        return pltpu.make_async_remote_copy(
            src_ref=src.at[span],
            dst_ref=out_ref.at[slot, span],
            send_sem=send_sem.at[sem, j],
            recv_sem=recv_sem.at[slot, j],
            device_id={"blocks": there},
            device_id_type=MESH,
        )

    def run(mate, far, side):
        beyond = (me + 2 * side >= 0) & (me + 2 * side < count)
        before = (me - 2 * side >= 0) & (me - 2 * side < count)
        away = (me + far >= 0) & (me + far < count)
        barrier = pltpu.get_barrier_semaphore()

        def signal(there):
            pl.semaphore_signal(barrier, inc=1, device_id={"blocks": there}, device_id_type=MESH)

        signal(me + mate)
        signal(me + side)
        pl.when(beyond)(lambda: signal(me + 2 * side))
        pl.when(before)(lambda: signal(me - 2 * side))
        pl.when(away)(lambda: signal(me + far))
        peers = 2 + beyond.astype(jnp.int32) + before.astype(jnp.int32) + away.astype(jnp.int32)
        pl.semaphore_wait(barrier, peers)

        def direct(j):
            return send(own_ref, mid - side, me + side, 0, j)

        def onward(j):
            return send(out_ref.at[mid + side], mid - side, me + 2 * side, 1, j)

        def long(j):
            return send(own_ref, mid - far, me + far, 2, j)

        def near(j):
            return send(own_ref, mid - mate, me + mate, 3, j)

        def pass_near(j):
            return send(out_ref.at[mid + side], mid + side - mate, me + mate, 4, j)

        def pass_back(j):
            return send(out_ref.at[mid - side], mid - side - mate, me + mate, 5, j)

        def landed(offset, j):
            return send(own_ref, mid + offset, me + mate, 0, j)

        for j in range(PARTS):
            direct(j).start()
            near(j).start()
        for j in range(PARTS):
            pl.when(away)(lambda: long(j).start())

        out_ref[mid] = own_ref[...]
        for offset in (-3, -2, -1, 1, 2, 3):
            if offset not in (mate, side):
                there = me + offset

                @pl.when((there < 0) | (there >= count))
                def _():
                    out_ref[mid + offset] = jnp.zeros(own_ref.shape, own_ref.dtype)

        for j in range(PARTS):
            landed(side, j).wait_recv()
            pl.when(beyond)(lambda: onward(j).start())
            pass_near(j).start()
        for j in range(PARTS):

            @pl.when(before)
            def _():
                landed(-side, j).wait_recv()
                pass_back(j).start()

        for j in range(PARTS):
            landed(mate, j).wait_recv()
            landed(side + mate, j).wait_recv()

            @pl.when(before)
            def _():
                landed(mate - side, j).wait_recv()
                pass_back(j).wait_send()

            @pl.when(beyond)
            def _():
                onward(j).wait_send()

            @pl.when(away)
            def _():
                landed(far, j).wait_recv()
                long(j).wait_send()

            pass_near(j).wait_send()
            direct(j).wait_send()
            near(j).wait_send()

    for mate, far in ((1, -3), (-1, 3)):
        for side in (2, -2):
            here = (odd == (0 if mate == 1 else 1)) & ((right if side < 0 else jnp.logical_not(right)))
            pl.when(here)(functools.partial(run, mate, far, side))


def view_kernel(
    dims, win_ref, img_ref, xm_ref, xt_ref, tap_ref, extra_ref, keep_ref, mate_ref, far_ref, held, low, mats
):
    views, rows, across, along, hops, margin = dims
    group = 16
    r = lax.broadcasted_iota(jnp.int32, (along, along), 0)
    c = lax.broadcasted_iota(jnp.int32, (along, along), 1)
    near = jnp.abs(r - c) <= margin

    @pl.loop(0, views)
    def _(v):
        for kind in range(4):
            line = jnp.broadcast_to(tap_ref[v, pl.ds(kind, 1), :], (along, along))
            turned = pltpu.roll(line, 0, 1, stride=1, stride_axis=0)
            mats[v, kind] = jnp.where(near, turned, 0.0).astype(BF16)

    @pl.loop(0, across // group)
    def _(g):
        base = pl.multiple_of(g * group, group)
        slabs = []
        for p in range(0, group, 2):
            pair = [win_ref[:, base + p + q].reshape(-1, along) for q in range(2)]
            res = jnp.dot(
                xm_ref[...], jnp.concatenate(pair, axis=1), preferred_element_type=F32
            ).astype(BF16)
            slabs += [res[:, :along], res[:, along:]]
        held[:, pl.ds(base, group), :] = jnp.swapaxes(jnp.stack(slabs), 0, 1)

    some = 8
    per = rows // some

    def both(left, block):
        outs = []
        for i in range(0, some, 2):
            pair = jnp.concatenate([block[i], block[i + 1]], axis=1)
            res = jnp.dot(left, pair, preferred_element_type=F32)
            outs += [res[:, :along], res[:, along:]]
        return outs

    @pl.loop(0, views * per)
    def _(t):
        v = t // per
        first = pl.multiple_of(t * some, some)
        inside = (t % per) * some
        block = held[pl.ds(first, some)].reshape(some * across, along)
        blur_z = jnp.dot(block, mats[v, 0], preferred_element_type=F32).astype(BF16)
        predicted = both(mats[v, 2], blur_z.reshape(some, across, along))
        ratios = []
        for i in range(some):
            image = img_ref[v, inside + i].astype(F32)
            ratios.append((image / (predicted[i] + extra_ref[first + i])).astype(BF16))
        ratio = jnp.concatenate(ratios, axis=0)
        back_z = jnp.dot(ratio, mats[v, 1], preferred_element_type=F32).astype(BF16)
        back = both(mats[v, 3], back_z.reshape(some, across, along))
        for i in range(some):
            top = back[i].astype(BF16)
            held[first + i] = top
            low[first + i] = (back[i] - top.astype(F32)).astype(BF16)

    @pl.loop(0, across // group)
    def _(g):
        base = pl.multiple_of(g * group, group)
        tops = jnp.swapaxes(held[:, pl.ds(base, group), :], 0, 1)
        lows = jnp.swapaxes(low[:, pl.ds(base, group), :], 0, 1)
        for p in range(0, group, 2):
            pair = [jnp.concatenate([tops[p + q], lows[p + q]], axis=0) for q in range(2)]
            both_p = jnp.dot(
                xt_ref[...], jnp.concatenate(pair, axis=1), preferred_element_type=F32
            )
            for q in range(2):
                res = both_p[:, q * along : (q + 1) * along].reshape(7, rows, along)
                for k in range(3):
                    keep_ref[k, base + p + q] = res[k]
                    mate_ref[k, base + p + q] = res[3 + k]
                far_ref[base + p + q] = res[6]


def vmem(n):
    return [pl.BlockSpec(memory_space=pltpu.VMEM)] * n


def taken(taps, index):
    match = index[..., None] == jnp.arange(taps.shape[-1])
    return jnp.sum(jnp.where(match, taps.astype(F32), 0.0), axis=-1)


def body(estimate, images, point_spread, shifts):
    views = images.shape[0]
    rows, across, along = estimate.shape
    taps = point_spread.shape[2]
    margin = taps // 2
    count = lax.axis_size("blocks")
    hops = -(-(margin + SHIFT) // rows)
    width = rows * (2 * hops + 1)
    slab = rows * count
    kernel = (point_spread / jnp.sum(point_spread, axis=2, keepdims=True)).astype(BF16)

    place = (jnp.arange(along) + along // 2) % along - along // 2
    plus = margin + place
    minus = margin - place
    lines = jnp.stack([minus, plus, plus, minus])
    which = jnp.stack([kernel[:, 2], kernel[:, 2], kernel[:, 1], kernel[:, 1]], axis=1)
    tap_lines = taken(which[:, :, None, :], lines[None])

    own = lax.axis_index("blocks") * rows + jnp.arange(rows)[None, :] - shifts[:, None]
    valid = (own >= 0) & (own < slab)
    index = (
        jnp.arange(width)[None, None, :]
        - jnp.arange(rows)[None, :, None]
        + shifts[:, None, None]
        + (margin - rows * hops)
    )
    x_mat = jnp.where(valid[:, :, None], taken(kernel[:, 0][:, None, None, :], index), 0.0)
    x_mat = x_mat.astype(BF16).reshape(views * rows, width)
    odd = lax.axis_index("blocks") % 2
    order = jnp.where(odd == 1, jnp.array([1, 3, 5, 0, 2, 4, 6]), jnp.array([1, 3, 5, 2, 4, 6, 0]))
    x_turned = x_mat.T.reshape(2 * hops + 1, rows, views * rows)[order].reshape(width, views * rows)
    x_twice = jnp.concatenate([x_turned, x_turned], axis=1)
    extra = jnp.where(valid, 0.0, 1.0).astype(F32).reshape(views * rows)

    block = (across, rows, along)
    mine = jnp.swapaxes(estimate.astype(BF16), 0, 1)
    window = pl.pallas_call(
        functools.partial(window_kernel, count),
        out_shape=jax.ShapeDtypeStruct((2 * hops + 1,) + block, BF16),
        in_specs=vmem(1),
        out_specs=vmem(1)[0],
        scratch_shapes=[
            pltpu.SemaphoreType.DMA((6, PARTS)),
            pltpu.SemaphoreType.DMA((2 * hops + 1, PARTS)),
        ],
        compiler_params=pltpu.CompilerParams(collective_id=0, has_side_effects=True),
        name="window",
    )(mine)

    dims = (views, rows, across, along, hops, margin)
    keep, mates, far = pl.pallas_call(
        functools.partial(view_kernel, dims),
        out_shape=(
            jax.ShapeDtypeStruct((3,) + block, F32),
            jax.ShapeDtypeStruct((3,) + block, F32),
            jax.ShapeDtypeStruct(block, F32),
        ),
        in_specs=vmem(5) + [pl.BlockSpec(memory_space=pltpu.SMEM)],
        out_specs=tuple(vmem(3)),
        scratch_shapes=[
            pltpu.VMEM((views * rows, across, along), BF16),
            pltpu.VMEM((views * rows, across, along), BF16),
            pltpu.VMEM((views, 4, along, along), BF16),
        ],
        compiler_params=pltpu.CompilerParams(vmem_limit_bytes=56 * 1024 * 1024),
        name="views",
    )(window, images, x_mat, x_twice, tap_lines, extra)


    def sent(value, step_of):
        pairs = [(i, i + step_of(i)) for i in range(count) if 0 <= i + step_of(i) < count]
        return lax.ppermute(value.astype(HALF), "blocks", pairs).astype(F32)

    away = sent(far, lambda i: 3 if i % 2 else -3)
    keep = keep + sent(mates, lambda i: -1 if i % 2 else 1)
    summed = keep[1] + away + sent(keep[0], lambda i: -2) + sent(keep[2], lambda i: 2)
    return estimate * jnp.swapaxes(summed, 0, 1) / views


def solution(mesh):
    in_specs = (
        P(("groups", "blocks"), None, None),
        P(None, ("groups", "blocks"), None, None),
        P(),
        P(),
    )
    out_specs = P(("groups", "blocks"), None, None)
    return jax.shard_map(body, mesh=mesh, in_specs=in_specs, out_specs=out_specs, check_vma=False)
```

```python
import functools

import jax
import jax.numpy as jnp
from jax import lax
from jax.experimental import pallas as pl
from jax.experimental.pallas import tpu as pltpu
from jax.sharding import PartitionSpec as P

SHIFT = 32
PARTS = 8
F32 = jnp.float32
BF16 = jnp.bfloat16
HALF = jnp.float16
MESH = pl.DeviceIdType.MESH


def window_kernel(count, own_ref, out_ref, send_sem, recv_sem):
    me = lax.axis_index("blocks")
    odd = lax.rem(me, 2)
    right = lax.rem(me, 4) >= 2
    mid = 3

    part = own_ref.shape[0] // PARTS

    def send(src, slot, there, sem, j):
        span = pl.ds(j * part, part)
        return pltpu.make_async_remote_copy(
            src_ref=src.at[span],
            dst_ref=out_ref.at[slot, span],
            send_sem=send_sem.at[sem, j],
            recv_sem=recv_sem.at[slot, j],
            device_id={"blocks": there},
            device_id_type=MESH,
        )

    def run(mate, far, side):
        beyond = (me + 2 * side >= 0) & (me + 2 * side < count)
        before = (me - 2 * side >= 0) & (me - 2 * side < count)
        away = (me + far >= 0) & (me + far < count)
        barrier = pltpu.get_barrier_semaphore()

        def signal(there):
            pl.semaphore_signal(barrier, inc=1, device_id={"blocks": there}, device_id_type=MESH)

        signal(me + mate)
        signal(me + side)
        pl.when(beyond)(lambda: signal(me + 2 * side))
        pl.when(before)(lambda: signal(me - 2 * side))
        pl.when(away)(lambda: signal(me + far))
        peers = 2 + beyond.astype(jnp.int32) + before.astype(jnp.int32) + away.astype(jnp.int32)
        pl.semaphore_wait(barrier, peers)

        def direct(j):
            return send(own_ref, mid - side, me + side, 0, j)

        def onward(j):
            return send(out_ref.at[mid + side], mid - side, me + 2 * side, 1, j)

        def long(j):
            return send(own_ref, mid - far, me + far, 2, j)

        def near(j):
            return send(own_ref, mid - mate, me + mate, 3, j)

        def pass_near(j):
            return send(out_ref.at[mid + side], mid + side - mate, me + mate, 4, j)

        def pass_back(j):
            return send(out_ref.at[mid - side], mid - side - mate, me + mate, 5, j)

        def landed(offset, j):
            return send(own_ref, mid + offset, me + mate, 0, j)

        for j in range(PARTS):
            direct(j).start()
            pl.when(away)(lambda: long(j).start())
            near(j).start()

        out_ref[mid] = own_ref[...]
        for offset in (-3, -2, -1, 1, 2, 3):
            if offset not in (mate, side):
                there = me + offset

                @pl.when((there < 0) | (there >= count))
                def _():
                    out_ref[mid + offset] = jnp.zeros(own_ref.shape, own_ref.dtype)

        for j in range(PARTS):
            landed(side, j).wait_recv()
            pl.when(beyond)(lambda: onward(j).start())
            pass_near(j).start()
        for j in range(PARTS):

            @pl.when(before)
            def _():
                landed(-side, j).wait_recv()
                pass_back(j).start()

        for j in range(PARTS):
            landed(mate, j).wait_recv()
            landed(side + mate, j).wait_recv()

            @pl.when(before)
            def _():
                landed(mate - side, j).wait_recv()
                pass_back(j).wait_send()

            @pl.when(beyond)
            def _():
                onward(j).wait_send()

            @pl.when(away)
            def _():
                landed(far, j).wait_recv()
                long(j).wait_send()

            pass_near(j).wait_send()
            direct(j).wait_send()
            near(j).wait_send()

    for mate, far in ((1, -3), (-1, 3)):
        for side in (2, -2):
            here = (odd == (0 if mate == 1 else 1)) & ((right if side < 0 else jnp.logical_not(right)))
            pl.when(here)(functools.partial(run, mate, far, side))


def view_kernel(
    dims, win_ref, img_ref, xm_ref, xt_ref, tap_ref, extra_ref, keep_ref, mate_ref, far_ref, held, low, mats
):
    views, rows, across, along, hops, margin = dims
    group = 16
    r = lax.broadcasted_iota(jnp.int32, (along, along), 0)
    c = lax.broadcasted_iota(jnp.int32, (along, along), 1)
    near = jnp.abs(r - c) <= margin

    @pl.loop(0, views)
    def _(v):
        for kind in range(4):
            line = jnp.broadcast_to(tap_ref[v, pl.ds(kind, 1), :], (along, along))
            turned = pltpu.roll(line, 0, 1, stride=1, stride_axis=0)
            mats[v, kind] = jnp.where(near, turned, 0.0).astype(BF16)

    @pl.loop(0, across // group)
    def _(g):
        base = pl.multiple_of(g * group, group)
        slabs = []
        for p in range(0, group, 2):
            pair = [win_ref[:, base + p + q].reshape(-1, along) for q in range(2)]
            res = jnp.dot(
                xm_ref[...], jnp.concatenate(pair, axis=1), preferred_element_type=F32
            ).astype(BF16)
            slabs += [res[:, :along], res[:, along:]]
        held[:, pl.ds(base, group), :] = jnp.swapaxes(jnp.stack(slabs), 0, 1)

    some = 16
    per = rows // some

    def both(left, block):
        outs = []
        for i in range(0, some, 2):
            pair = jnp.concatenate([block[i], block[i + 1]], axis=1)
            res = jnp.dot(left, pair, preferred_element_type=F32)
            outs += [res[:, :along], res[:, along:]]
        return outs

    @pl.loop(0, views * per)
    def _(t):
        v = t // per
        first = pl.multiple_of(t * some, some)
        inside = (t % per) * some
        block = held[pl.ds(first, some)].reshape(some * across, along)
        blur_z = jnp.dot(block, mats[v, 0], preferred_element_type=F32).astype(BF16)
        predicted = both(mats[v, 2], blur_z.reshape(some, across, along))
        ratios = []
        for i in range(some):
            image = img_ref[v, inside + i].astype(F32)
            ratios.append((image / (predicted[i] + extra_ref[first + i])).astype(BF16))
        ratio = jnp.concatenate(ratios, axis=0)
        back_z = jnp.dot(ratio, mats[v, 1], preferred_element_type=F32).astype(BF16)
        back = both(mats[v, 3], back_z.reshape(some, across, along))
        for i in range(some):
            top = back[i].astype(BF16)
            held[first + i] = top
            low[first + i] = (back[i] - top.astype(F32)).astype(BF16)

    @pl.loop(0, across // group)
    def _(g):
        base = pl.multiple_of(g * group, group)
        tops = jnp.swapaxes(held[:, pl.ds(base, group), :], 0, 1)
        lows = jnp.swapaxes(low[:, pl.ds(base, group), :], 0, 1)
        for p in range(0, group, 2):
            pair = [jnp.concatenate([tops[p + q], lows[p + q]], axis=0) for q in range(2)]
            both_p = jnp.dot(
                xt_ref[...], jnp.concatenate(pair, axis=1), preferred_element_type=F32
            )
            for q in range(2):
                res = both_p[:, q * along : (q + 1) * along].reshape(7, rows, along)
                for k in range(3):
                    keep_ref[k, base + p + q] = res[k]
                    mate_ref[k, base + p + q] = res[3 + k]
                far_ref[base + p + q] = res[6]


def vmem(n):
    return [pl.BlockSpec(memory_space=pltpu.VMEM)] * n


def taken(taps, index):
    match = index[..., None] == jnp.arange(taps.shape[-1])
    return jnp.sum(jnp.where(match, taps.astype(F32), 0.0), axis=-1)


def body(estimate, images, point_spread, shifts):
    views = images.shape[0]
    rows, across, along = estimate.shape
    taps = point_spread.shape[2]
    margin = taps // 2
    count = lax.axis_size("blocks")
    hops = -(-(margin + SHIFT) // rows)
    width = rows * (2 * hops + 1)
    slab = rows * count
    kernel = (point_spread / jnp.sum(point_spread, axis=2, keepdims=True)).astype(BF16)

    place = (jnp.arange(along) + along // 2) % along - along // 2
    plus = margin + place
    minus = margin - place
    lines = jnp.stack([minus, plus, plus, minus])
    which = jnp.stack([kernel[:, 2], kernel[:, 2], kernel[:, 1], kernel[:, 1]], axis=1)
    tap_lines = taken(which[:, :, None, :], lines[None])

    own = lax.axis_index("blocks") * rows + jnp.arange(rows)[None, :] - shifts[:, None]
    valid = (own >= 0) & (own < slab)
    index = (
        jnp.arange(width)[None, None, :]
        - jnp.arange(rows)[None, :, None]
        + shifts[:, None, None]
        + (margin - rows * hops)
    )
    x_mat = jnp.where(valid[:, :, None], taken(kernel[:, 0][:, None, None, :], index), 0.0)
    x_mat = x_mat.astype(BF16).reshape(views * rows, width)
    odd = lax.axis_index("blocks") % 2
    order = jnp.where(odd == 1, jnp.array([1, 3, 5, 0, 2, 4, 6]), jnp.array([1, 3, 5, 2, 4, 6, 0]))
    x_turned = x_mat.T.reshape(2 * hops + 1, rows, views * rows)[order].reshape(width, views * rows)
    x_twice = jnp.concatenate([x_turned, x_turned], axis=1)
    extra = jnp.where(valid, 0.0, 1.0).astype(F32).reshape(views * rows)

    block = (across, rows, along)
    mine = jnp.swapaxes(estimate.astype(BF16), 0, 1)
    window = pl.pallas_call(
        functools.partial(window_kernel, count),
        out_shape=jax.ShapeDtypeStruct((2 * hops + 1,) + block, BF16),
        in_specs=vmem(1),
        out_specs=vmem(1)[0],
        scratch_shapes=[
            pltpu.SemaphoreType.DMA((6, PARTS)),
            pltpu.SemaphoreType.DMA((2 * hops + 1, PARTS)),
        ],
        compiler_params=pltpu.CompilerParams(collective_id=0, has_side_effects=True),
        name="window",
    )(mine)

    dims = (views, rows, across, along, hops, margin)
    keep, mates, far = pl.pallas_call(
        functools.partial(view_kernel, dims),
        out_shape=(
            jax.ShapeDtypeStruct((3,) + block, F32),
            jax.ShapeDtypeStruct((3,) + block, F32),
            jax.ShapeDtypeStruct(block, F32),
        ),
        in_specs=vmem(5) + [pl.BlockSpec(memory_space=pltpu.SMEM)],
        out_specs=tuple(vmem(3)),
        scratch_shapes=[
            pltpu.VMEM((views * rows, across, along), BF16),
            pltpu.VMEM((views * rows, across, along), BF16),
            pltpu.VMEM((views, 4, along, along), BF16),
        ],
        compiler_params=pltpu.CompilerParams(vmem_limit_bytes=56 * 1024 * 1024),
        name="views",
    )(window, images, x_mat, x_twice, tap_lines, extra)


    def sent(value, step_of):
        pairs = [(i, i + step_of(i)) for i in range(count) if 0 <= i + step_of(i) < count]
        return lax.ppermute(value.astype(HALF), "blocks", pairs).astype(F32)

    away = sent(far, lambda i: 3 if i % 2 else -3)
    keep = keep + sent(mates, lambda i: -1 if i % 2 else 1)
    summed = keep[1] + away + sent(keep[0], lambda i: -2) + sent(keep[2], lambda i: 2)
    return estimate * jnp.swapaxes(summed, 0, 1) / views


def solution(mesh):
    in_specs = (
        P(("groups", "blocks"), None, None),
        P(None, ("groups", "blocks"), None, None),
        P(),
        P(),
    )
    out_specs = P(("groups", "blocks"), None, None)
    return jax.shard_map(body, mesh=mesh, in_specs=in_specs, out_specs=out_specs, check_vma=False)
```

```python
import functools

import jax
import jax.numpy as jnp
from jax import lax
from jax.experimental import pallas as pl
from jax.experimental.pallas import tpu as pltpu
from jax.sharding import PartitionSpec as P

SHIFT = 32
PARTS = 8
F32 = jnp.float32
BF16 = jnp.bfloat16
HALF = jnp.float16
MESH = pl.DeviceIdType.MESH


def window_kernel(count, own_ref, out_ref, send_sem, recv_sem):
    me = lax.axis_index("blocks")
    odd = lax.rem(me, 2)
    right = lax.rem(me, 4) >= 2
    mid = 3

    part = own_ref.shape[0] // PARTS

    def send(src, slot, there, sem, j):
        span = pl.ds(j * part, part)
        return pltpu.make_async_remote_copy(
            src_ref=src.at[span],
            dst_ref=out_ref.at[slot, span],
            send_sem=send_sem.at[sem, j],
            recv_sem=recv_sem.at[slot, j],
            device_id={"blocks": there},
            device_id_type=MESH,
        )

    def run(mate, far, side):
        beyond = (me + 2 * side >= 0) & (me + 2 * side < count)
        before = (me - 2 * side >= 0) & (me - 2 * side < count)
        away = (me + far >= 0) & (me + far < count)
        barrier = pltpu.get_barrier_semaphore()

        def signal(there):
            pl.semaphore_signal(barrier, inc=1, device_id={"blocks": there}, device_id_type=MESH)

        signal(me + mate)
        signal(me + side)
        pl.when(beyond)(lambda: signal(me + 2 * side))
        pl.when(before)(lambda: signal(me - 2 * side))
        pl.when(away)(lambda: signal(me + far))
        peers = 2 + beyond.astype(jnp.int32) + before.astype(jnp.int32) + away.astype(jnp.int32)
        pl.semaphore_wait(barrier, peers)

        def direct(j):
            return send(own_ref, mid - side, me + side, 0, j)

        def onward(j):
            return send(out_ref.at[mid + side], mid - side, me + 2 * side, 1, j)

        def long(j):
            return send(own_ref, mid - far, me + far, 2, j)

        def near(j):
            return send(own_ref, mid - mate, me + mate, 3, j)

        def pass_near(j):
            return send(out_ref.at[mid + side], mid + side - mate, me + mate, 4, j)

        def pass_back(j):
            return send(out_ref.at[mid - side], mid - side - mate, me + mate, 5, j)

        def landed(offset, j):
            return send(own_ref, mid + offset, me + mate, 0, j)

        for j in range(PARTS):
            direct(j).start()
            pl.when(away)(lambda: long(j).start())
            near(j).start()

        out_ref[mid] = own_ref[...]
        for offset in (-3, -2, -1, 1, 2, 3):
            if offset not in (mate, side):
                there = me + offset

                @pl.when((there < 0) | (there >= count))
                def _():
                    out_ref[mid + offset] = jnp.zeros(own_ref.shape, own_ref.dtype)

        for j in range(PARTS):
            landed(side, j).wait_recv()
            pl.when(beyond)(lambda: onward(j).start())
            pass_near(j).start()
        for j in range(PARTS):

            @pl.when(before)
            def _():
                landed(-side, j).wait_recv()
                pass_back(j).start()

        for j in range(PARTS):
            landed(mate, j).wait_recv()
            landed(side + mate, j).wait_recv()

            @pl.when(before)
            def _():
                landed(mate - side, j).wait_recv()
                pass_back(j).wait_send()

            @pl.when(beyond)
            def _():
                onward(j).wait_send()

            @pl.when(away)
            def _():
                landed(far, j).wait_recv()
                long(j).wait_send()

            pass_near(j).wait_send()
            direct(j).wait_send()
            near(j).wait_send()

    for mate, far in ((1, -3), (-1, 3)):
        for side in (2, -2):
            here = (odd == (0 if mate == 1 else 1)) & ((right if side < 0 else jnp.logical_not(right)))
            pl.when(here)(functools.partial(run, mate, far, side))


def view_kernel(
    dims, win_ref, img_ref, xm_ref, xt_ref, tap_ref, extra_ref, keep_ref, mate_ref, far_ref, held, low, mats
):
    views, rows, across, along, hops, margin = dims
    group = 32
    r = lax.broadcasted_iota(jnp.int32, (along, along), 0)
    c = lax.broadcasted_iota(jnp.int32, (along, along), 1)
    near = jnp.abs(r - c) <= margin

    @pl.loop(0, views)
    def _(v):
        for kind in range(4):
            line = jnp.broadcast_to(tap_ref[v, pl.ds(kind, 1), :], (along, along))
            turned = pltpu.roll(line, 0, 1, stride=1, stride_axis=0)
            mats[v, kind] = jnp.where(near, turned, 0.0).astype(BF16)

    @pl.loop(0, across // group)
    def _(g):
        base = pl.multiple_of(g * group, group)
        slabs = []
        for p in range(0, group, 2):
            pair = [win_ref[:, base + p + q].reshape(-1, along) for q in range(2)]
            res = jnp.dot(
                xm_ref[...], jnp.concatenate(pair, axis=1), preferred_element_type=F32
            ).astype(BF16)
            slabs += [res[:, :along], res[:, along:]]
        held[:, pl.ds(base, group), :] = jnp.swapaxes(jnp.stack(slabs), 0, 1)

    some = 16
    per = rows // some

    def both(left, block):
        outs = []
        for i in range(0, some, 2):
            pair = jnp.concatenate([block[i], block[i + 1]], axis=1)
            res = jnp.dot(left, pair, preferred_element_type=F32)
            outs += [res[:, :along], res[:, along:]]
        return outs

    @pl.loop(0, views * per)
    def _(t):
        v = t // per
        first = pl.multiple_of(t * some, some)
        inside = (t % per) * some
        block = held[pl.ds(first, some)].reshape(some * across, along)
        blur_z = jnp.dot(block, mats[v, 0], preferred_element_type=F32).astype(BF16)
        predicted = both(mats[v, 2], blur_z.reshape(some, across, along))
        ratios = []
        for i in range(some):
            image = img_ref[v, inside + i].astype(F32)
            ratios.append((image / (predicted[i] + extra_ref[first + i])).astype(BF16))
        ratio = jnp.concatenate(ratios, axis=0)
        back_z = jnp.dot(ratio, mats[v, 1], preferred_element_type=F32).astype(BF16)
        back = both(mats[v, 3], back_z.reshape(some, across, along))
        for i in range(some):
            top = back[i].astype(BF16)
            held[first + i] = top
            low[first + i] = (back[i] - top.astype(F32)).astype(BF16)

    @pl.loop(0, across // group)
    def _(g):
        base = pl.multiple_of(g * group, group)
        tops = jnp.swapaxes(held[:, pl.ds(base, group), :], 0, 1)
        lows = jnp.swapaxes(low[:, pl.ds(base, group), :], 0, 1)
        for p in range(0, group, 2):
            pair = [jnp.concatenate([tops[p + q], lows[p + q]], axis=0) for q in range(2)]
            both_p = jnp.dot(
                xt_ref[...], jnp.concatenate(pair, axis=1), preferred_element_type=F32
            )
            for q in range(2):
                res = both_p[:, q * along : (q + 1) * along].reshape(7, rows, along)
                for k in range(3):
                    keep_ref[k, base + p + q] = res[k]
                    mate_ref[k, base + p + q] = res[3 + k]
                far_ref[base + p + q] = res[6]


def vmem(n):
    return [pl.BlockSpec(memory_space=pltpu.VMEM)] * n


def taken(taps, index):
    match = index[..., None] == jnp.arange(taps.shape[-1])
    return jnp.sum(jnp.where(match, taps.astype(F32), 0.0), axis=-1)


def body(estimate, images, point_spread, shifts):
    views = images.shape[0]
    rows, across, along = estimate.shape
    taps = point_spread.shape[2]
    margin = taps // 2
    count = lax.axis_size("blocks")
    hops = -(-(margin + SHIFT) // rows)
    width = rows * (2 * hops + 1)
    slab = rows * count
    kernel = (point_spread / jnp.sum(point_spread, axis=2, keepdims=True)).astype(BF16)

    place = (jnp.arange(along) + along // 2) % along - along // 2
    plus = margin + place
    minus = margin - place
    lines = jnp.stack([minus, plus, plus, minus])
    which = jnp.stack([kernel[:, 2], kernel[:, 2], kernel[:, 1], kernel[:, 1]], axis=1)
    tap_lines = taken(which[:, :, None, :], lines[None])

    own = lax.axis_index("blocks") * rows + jnp.arange(rows)[None, :] - shifts[:, None]
    valid = (own >= 0) & (own < slab)
    index = (
        jnp.arange(width)[None, None, :]
        - jnp.arange(rows)[None, :, None]
        + shifts[:, None, None]
        + (margin - rows * hops)
    )
    x_mat = jnp.where(valid[:, :, None], taken(kernel[:, 0][:, None, None, :], index), 0.0)
    x_mat = x_mat.astype(BF16).reshape(views * rows, width)
    odd = lax.axis_index("blocks") % 2
    order = jnp.where(odd == 1, jnp.array([1, 3, 5, 0, 2, 4, 6]), jnp.array([1, 3, 5, 2, 4, 6, 0]))
    x_turned = x_mat.T.reshape(2 * hops + 1, rows, views * rows)[order].reshape(width, views * rows)
    x_twice = jnp.concatenate([x_turned, x_turned], axis=1)
    extra = jnp.where(valid, 0.0, 1.0).astype(F32).reshape(views * rows)

    block = (across, rows, along)
    mine = jnp.swapaxes(estimate.astype(BF16), 0, 1)
    window = pl.pallas_call(
        functools.partial(window_kernel, count),
        out_shape=jax.ShapeDtypeStruct((2 * hops + 1,) + block, BF16),
        in_specs=vmem(1),
        out_specs=vmem(1)[0],
        scratch_shapes=[
            pltpu.SemaphoreType.DMA((6, PARTS)),
            pltpu.SemaphoreType.DMA((2 * hops + 1, PARTS)),
        ],
        compiler_params=pltpu.CompilerParams(collective_id=0, has_side_effects=True),
        name="window",
    )(mine)

    dims = (views, rows, across, along, hops, margin)
    keep, mates, far = pl.pallas_call(
        functools.partial(view_kernel, dims),
        out_shape=(
            jax.ShapeDtypeStruct((3,) + block, F32),
            jax.ShapeDtypeStruct((3,) + block, F32),
            jax.ShapeDtypeStruct(block, F32),
        ),
        in_specs=vmem(5) + [pl.BlockSpec(memory_space=pltpu.SMEM)],
        out_specs=tuple(vmem(3)),
        scratch_shapes=[
            pltpu.VMEM((views * rows, across, along), BF16),
            pltpu.VMEM((views * rows, across, along), BF16),
            pltpu.VMEM((views, 4, along, along), BF16),
        ],
        compiler_params=pltpu.CompilerParams(vmem_limit_bytes=56 * 1024 * 1024),
        name="views",
    )(window, images, x_mat, x_twice, tap_lines, extra)


    def sent(value, step_of):
        pairs = [(i, i + step_of(i)) for i in range(count) if 0 <= i + step_of(i) < count]
        return lax.ppermute(value.astype(HALF), "blocks", pairs).astype(F32)

    away = sent(far, lambda i: 3 if i % 2 else -3)
    keep = keep + sent(mates, lambda i: -1 if i % 2 else 1)
    summed = keep[1] + away + sent(keep[0], lambda i: -2) + sent(keep[2], lambda i: 2)
    return estimate * jnp.swapaxes(summed, 0, 1) / views


def solution(mesh):
    in_specs = (
        P(("groups", "blocks"), None, None),
        P(None, ("groups", "blocks"), None, None),
        P(),
        P(),
    )
    out_specs = P(("groups", "blocks"), None, None)
    return jax.shard_map(body, mesh=mesh, in_specs=in_specs, out_specs=out_specs, check_vma=False)
```
